128 devices in a mesh: dom: 16 (over y_lo, z, core), rep: 8 (over y_hi, x).
Axes of the slice: x: 4, y: 4 (y_hi: 2, y_lo: 2; y = y_hi * 2 + y_lo), z: 4, core: 2. Of those that a mesh axis runs over, the one named last changes fastest.
Arguments:
- node_features: bfloat16 [65536, 256], P(('dom', 'rep')), may hold values from -6 to 6
- weight: bfloat16 [256, 256], replicated, may hold values from -0.375 to 0.375
- cotangent: bfloat16 [65536, 256], P(('dom', 'rep')), may hold values from -6 to 6
- tile_row: int32 [16, 8, 512], P('dom', 'rep'), may hold values from 0 to 31
- tile_col: int32 [16, 8, 512], P('dom', 'rep'), may hold values from 0 to 63
- tile_values: bfloat16 [16, 8, 512, 128, 128], P('dom', 'rep'), may hold values from -0.0625 to 0.0625
- tile_count: int32 [16, 8], P('dom', 'rep'), may hold values from 128 to 512, as said below
Outputs:
- output: bfloat16 [65536, 256], P(('dom', 'rep'))
- grad_features: bfloat16 [65536, 256], P(('dom', 'rep'))
- grad_weight: float32 [256, 256], replicated
The draws below stay inside these ranges and needn't reach their ends.
Inputs may be any that keep to these rules, and one draw needn't show every extreme that they name: Live slots are the first tile_count slots of each device's list; some device has all 512 slots live.
All inputs are finite; a program needn't handle non-finite values.
Results may differ from the reference program's by a relative error of at most 0.0061.
Values may be sent and summed in bfloat16 or wider, within the bound.
No kernel may reach another device: no remote copies, remote signals or barrier semaphores. Data moves between devices by JAX's collectives and lax.ppermute only.
A program may use at most 192 MiB of HBM per device.

```python
import jax
import jax.numpy as jnp
from jax import lax

F = 256
S = 4
K = 512
NODES = 65536
N_DOM = 16
N_REP = 8


def draw_tile_count(key, part):
    counts = jax.random.randint(jax.random.fold_in(key, 11), (N_DOM * N_REP,), K // 4, K + 1)
    fullest = jax.random.randint(jax.random.fold_in(key, 12), (), 0, N_DOM * N_REP)
    counts = jnp.where(jnp.arange(N_DOM * N_REP) == fullest, K, counts)
    return counts.reshape(N_DOM, N_REP).astype(jnp.int32)


def place_ends(drawn, key, least, largest):
    longest = drawn.shape.index(max(drawn.shape))
    spots = []
    for shift in (0, 1):
        where = [jax.random.randint(jax.random.fold_in(key, axis), (), 0, length) for axis, length in enumerate(drawn.shape)]
        where[longest] = (where[longest] + shift) % drawn.shape[longest]
        spots.append(tuple(where))
    return drawn.at[spots[0]].set(least).at[spots[1]].set(largest)


def steps_of(stream_key, shape, pieces, least, largest):
    loudness, own = 1.0, jax.random.fold_in(stream_key, 6)
    for position, parts in pieces:
        steps = jnp.exp(jax.random.uniform(jax.random.fold_in(own, position), (parts,), jnp.float32, least / len(pieces), largest / len(pieces)))
        loudness = loudness * jnp.repeat(steps, shape[position] // parts).reshape([-1 if axis == position else 1 for axis in range(len(shape))])
    return loudness


def centred(key, shape, deviation, reach, split=(), held_as=jnp.bfloat16):
    gain = steps_of(key, shape, split, -0.22, 0.18) if split else 1.0
    result = jax.random.normal(key, shape, jnp.float32) * deviation * gain
    return jnp.minimum(jnp.maximum(result, -reach), reach).astype(held_as)


def setup_inputs(seed: int = 0) -> dict:
    streams_of = jax.random.split(jax.random.key(seed), 8)
    node_features = centred(streams_of[0], (NODES, F), 1.0, 6.0, ((0, 128),))
    weight = centred(streams_of[1], (F, F), F ** -0.5, 0.375)
    cotangent = centred(streams_of[2], (NODES, F), 1.0, 6.0, ((0, 128),))
    tile_row = place_ends(jax.random.randint(streams_of[3], (N_DOM, N_REP, K), 0, N_REP * S), jax.random.fold_in(streams_of[3], 1), 0, (N_REP * S) - 1).astype(jnp.int32)
    tile_col = place_ends(jax.random.randint(streams_of[4], (N_DOM, N_REP, K), 0, N_DOM * S), jax.random.fold_in(streams_of[4], 1), 0, (N_DOM * S) - 1).astype(jnp.int32)
    tile_values = centred(streams_of[5], (N_DOM, N_REP, K, 128, 128), (16 * K) ** -0.5, 0.0625, ((0, 16), (1, 8)))
    tile_count = draw_tile_count(jax.random.fold_in(streams_of[7], 71), 0)
    return dict(node_features=node_features, weight=weight, cotangent=cotangent, tile_row=tile_row, tile_col=tile_col, tile_values=tile_values, tile_count=tile_count)


def silu_slope(summed):
    sig = jax.nn.sigmoid(summed)
    return sig * (1.0 + summed * (1.0 - sig))


def spread(source, values, pick, place, active, flipped, total_blocks):
    pattern = "tba,tbf->taf" if flipped else "tab,tbf->taf"

    def one_device(accum, items):
        tiles, pick_index, place_index, enabled = items
        picked = source[pick_index].astype(jnp.float32)
        products = jnp.einsum(pattern, tiles.astype(jnp.float32), picked)
        products = products * enabled.astype(jnp.float32)[:, None, None]
        return accum.at[place_index].add(products), None

    start = jnp.zeros((total_blocks, 128, source.shape[2]), jnp.float32)
    accum, unused = lax.scan(one_device, start, (values, pick, place, active))
    return accum


def reference(node_features, weight, cotangent, tile_row, tile_col, tile_values, tile_count):
    blocks_part = N_REP * S
    total_blocks = NODES // 128
    projected = jnp.dot(node_features, weight, preferred_element_type=jnp.float32).astype(jnp.bfloat16)
    source = projected.reshape(total_blocks, 128, F)
    part_index = jnp.arange(N_DOM, dtype=jnp.int32)[:, None, None]
    repl_index = jnp.arange(N_REP, dtype=jnp.int32)[None, :, None]
    global_row = (part_index * blocks_part + tile_row).reshape(N_DOM * N_REP, K).astype(jnp.int32)
    global_col = ((tile_col // S) * blocks_part + repl_index * S + tile_col % S).reshape(N_DOM * N_REP, K).astype(jnp.int32)
    active = (jnp.arange(K, dtype=jnp.int32)[None, None, :] < tile_count[:, :, None]).reshape(N_DOM * N_REP, K)
    values = tile_values.reshape(N_DOM * N_REP, K, 128, 128)
    summed = spread(source, values, global_col, global_row, active, False, total_blocks).reshape(NODES, F)
    output = jax.nn.silu(summed).astype(jnp.bfloat16)
    grad_summed = (cotangent.astype(jnp.float32) * silu_slope(summed)).astype(jnp.bfloat16)
    back = spread(grad_summed.reshape(total_blocks, 128, F), values, global_row, global_col, active, True, total_blocks)
    grad_projected = back.reshape(NODES, F).astype(jnp.bfloat16)
    grad_features = jnp.dot(grad_projected, weight.T, preferred_element_type=jnp.float32).astype(jnp.bfloat16)
    grad_weight = jnp.dot(node_features.T, grad_projected, preferred_element_type=jnp.float32)
    return output, grad_features, grad_weight
```

```python
import functools

import jax
import jax.numpy as jnp
from jax import lax
from jax.experimental import pallas as pl
from jax.experimental.pallas import tpu as pltpu
from jax.sharding import PartitionSpec as P

BLOCK = 128
UNROLL = 16


def pair_plan(place, pick, count, places, pairs_max):
    slots = place.shape[0]
    slot = jnp.arange(slots, dtype=jnp.int32)
    live = slot < count
    key = jnp.where(live, place, places)
    earlier = (key[:, None] == key[None, :]) & (slot[None, :] < slot[:, None])
    rank = jnp.sum(earlier, axis=1, dtype=jnp.int32)
    block = jnp.arange(places, dtype=jnp.int32)
    per_block = jnp.sum(key[None, :] == block[:, None], axis=1, dtype=jnp.int32)
    pairs = (per_block + 1) // 2
    before = jnp.sum(jnp.where(block[None, :] < block[:, None], pairs[None, :], 0), axis=1, dtype=jnp.int32)
    first = jnp.sum(jnp.where(key[:, None] == block[None, :], before[None, :], 0), axis=1, dtype=jnp.int32)
    position = jnp.where(live, 2 * first + rank, -1)
    half = jnp.arange(2 * pairs_max, dtype=jnp.int32)
    hit = half[:, None] == position[None, :]
    tile = jnp.sum(jnp.where(hit, slot[None, :] - slots, 0), axis=1, dtype=jnp.int32) + slots
    picked = jnp.sum(jnp.where(hit, pick[None, :], 0), axis=1, dtype=jnp.int32)
    placed = jnp.sum(jnp.where(hit, place[None, :], 0), axis=1, dtype=jnp.int32)
    return jnp.sum(pairs).reshape(1), tile, picked, placed


def load_kernel(tiles_ref, held_ref, sems):
    slots = tiles_ref.shape[0]
    pieces = sems.shape[0]
    piece = slots // pieces

    def copy(i):
        window = pl.ds(i * piece, piece)
        return pltpu.make_async_copy(tiles_ref.at[window], held_ref.at[window], sems.at[i])

    for i in range(pieces):
        copy(i).start()
    held_ref[slots] = jnp.zeros(held_ref.shape[1:], held_ref.dtype)
    for i in range(pieces):
        copy(i).wait()


def load_tiles(tiles):
    slots = tiles.shape[0]
    return pl.pallas_call(
        load_kernel,
        out_shape=pltpu.VMEM((slots + 1, BLOCK, BLOCK), tiles.dtype),
        in_specs=[pl.BlockSpec(memory_space=pl.ANY)],
        out_specs=pl.BlockSpec(memory_space=pltpu.VMEM),
        scratch_shapes=[pltpu.SemaphoreType.DMA((8,))],
        compiler_params=pltpu.CompilerParams(vmem_limit_bytes=1 << 20),
        cost_estimate=pl.CostEstimate(flops=0, bytes_accessed=2 * tiles.size, transcendentals=0),
        name="load_tiles",
    )(tiles)


def spread_kernel(flipped, pairs_ref, tile_ref, pick_ref, place_ref, tiles_ref, source_ref, *refs):
    *out_refs, total_ref = refs
    total_ref[...] = jnp.zeros_like(total_ref)

    def rows_of(index):
        return source_ref[pl.ds(pl.multiple_of(index * 64, 64), BLOCK), :]

    @pl.loop(0, (pairs_ref[0] + UNROLL - 1) // UNROLL)
    def _(turn):
        for step in range(UNROLL):
            first = (turn * UNROLL + step) * 2
            rows = jnp.concatenate([rows_of(pick_ref[first]), rows_of(pick_ref[first + 1])], axis=0)
            tiles = [tiles_ref[tile_ref[first]], tiles_ref[tile_ref[first + 1]]]
            if flipped:
                product = lax.dot_general(
                    jnp.concatenate(tiles, axis=0), rows, (((0,), (0,)), ((), ())), preferred_element_type=jnp.float32
                )
            else:
                product = jnp.dot(jnp.concatenate(tiles, axis=1), rows, preferred_element_type=jnp.float32)
            total_ref[place_ref[first]] += product

    part = total_ref.shape[0] // len(out_refs)
    for i, out_ref in enumerate(out_refs):
        out_ref[...] = total_ref[i * part : (i + 1) * part].astype(out_ref.dtype)


def spread(plan, tiles, source, places, parts, flipped):
    width = source.shape[1]
    return pl.pallas_call(
        functools.partial(spread_kernel, flipped),
        out_shape=[jax.ShapeDtypeStruct((places // parts, BLOCK, width), jnp.bfloat16)] * parts,
        in_specs=[pl.BlockSpec(memory_space=pltpu.SMEM)] * 4 + [pl.BlockSpec(memory_space=pltpu.VMEM)] * 2,
        out_specs=[pl.BlockSpec(memory_space=pltpu.VMEM)] * parts,
        scratch_shapes=[pltpu.VMEM((places, BLOCK, width), jnp.float32)],
        compiler_params=pltpu.CompilerParams(vmem_limit_bytes=24 << 20),
        cost_estimate=pl.CostEstimate(
            flops=2 * tiles.size * width, bytes_accessed=2 * (tiles.size + source.size), transcendentals=0
        ),
        name="spread_back" if flipped else "spread_forward",
    )(*plan, tiles, source)


def split(value):
    high = value.astype(jnp.bfloat16)
    return high, (value - high.astype(jnp.float32)).astype(jnp.bfloat16)


def middle_kernel(parts_ref, weight_ref, cotangent_ref, out_ref, send_ref):
    members, rows, width = parts_ref.shape
    share = width // members
    mixed = parts_ref[0].astype(jnp.float32)
    for member in range(1, members):
        mixed += parts_ref[member].astype(jnp.float32)
    high, low = split(mixed)
    weight = weight_ref[...]
    summed = jnp.dot(high, weight, preferred_element_type=jnp.float32)
    summed += jnp.dot(low, weight, preferred_element_type=jnp.float32)
    sig = jax.nn.sigmoid(summed)
    out_ref[...] = (summed * sig).astype(out_ref.dtype)
    slope = sig * (1.0 + summed * (1.0 - sig))
    grad = (cotangent_ref[...].astype(jnp.float32) * slope).astype(jnp.bfloat16)
    across = (((0,), (0,)), ((), ()))
    term = lax.dot_general(high, grad, across, preferred_element_type=jnp.float32)
    term += lax.dot_general(low, grad, across, preferred_element_type=jnp.float32)
    term_high, term_low = split(term)
    for member in range(members):
        mine = slice(member * share, (member + 1) * share)
        send_ref[member, :rows, :] = grad
        send_ref[member, rows : rows + share, :] = term_high[mine]
        send_ref[member, rows + share :, :] = term_low[mine]


def join_kernel(own_ref, other_ref, term_ref, send_ref):
    rows = own_ref.shape[1]
    share = term_ref.shape[0]
    send_ref[0, :rows, :] = (own_ref[0].astype(jnp.float32) + other_ref[0].astype(jnp.float32)).astype(jnp.bfloat16)
    high, low = split(term_ref[...])
    send_ref[0, rows : rows + share, :] = high
    send_ref[0, rows + share :, :] = low


def last_kernel(parts_ref, weight_ref, out_ref, term_ref):
    members = parts_ref.shape[0]
    rows = out_ref.shape[0]
    share = term_ref.shape[1]
    total = parts_ref[0].astype(jnp.float32)
    for member in range(1, members):
        total += parts_ref[member].astype(jnp.float32)
    grad = total[:rows].astype(jnp.bfloat16)
    out_ref[...] = lax.dot_general(
        grad, weight_ref[...], (((1,), (1,)), ((), ())), preferred_element_type=jnp.float32
    ).astype(out_ref.dtype)
    term = total[rows : rows + share] + total[rows + share :]
    for member in range(term_ref.shape[0]):
        term_ref[member] = term


def body(node_features, weight, cotangent, tile_row, tile_col, tile_values, tile_count):
    rows, width = node_features.shape
    dom_size = lax.axis_size("dom")
    rep_size = lax.axis_size("rep")
    slots = tile_row.shape[2]
    own = rows // BLOCK
    share = width // rep_size
    wide = rows + 2 * share
    params = pltpu.CompilerParams(vmem_limit_bytes=24 << 20)
    row_index = tile_row.reshape(slots)
    col_index = tile_col.reshape(slots)
    count = tile_count.reshape(())
    tiles = load_tiles(tile_values.reshape(slots, BLOCK, BLOCK))
    parity = lax.axis_index("dom") % 2

    gathered = lax.all_gather(node_features, "dom", axis=0, tiled=True)

    row_blocks = rep_size * own
    col_blocks = dom_size * own

    def padded(places):
        return -(-((slots + places) // 2) // UNROLL) * UNROLL

    forward_plan = pair_plan(row_index, col_index * (BLOCK // 64), count, row_blocks, padded(row_blocks))
    owner = col_index // own
    col_place = ((owner + parity) % 2) * (col_blocks // 2) + (owner // 2) * own + col_index % own
    row_pick = (row_index // own) * (wide // 64) + (row_index % own) * (BLOCK // 64)
    back_plan = pair_plan(col_place, row_pick, count, col_blocks, padded(col_blocks))

    (partial,) = spread(forward_plan, tiles, gathered, row_blocks, 1, False)
    parts = lax.all_to_all(partial.reshape(rep_size, rows, width), "rep", 0, 0, tiled=True)
    output, grads_out = pl.pallas_call(
        middle_kernel,
        out_shape=(
            jax.ShapeDtypeStruct((rows, width), jnp.bfloat16),
            jax.ShapeDtypeStruct((rep_size, wide, width), jnp.bfloat16),
        ),
        compiler_params=params,
        name="middle",
    )(parts, weight, cotangent)
    grads = lax.all_to_all(grads_out, "rep", 0, 0, tiled=True)

    term = jnp.sum(grads[:, rows:].astype(jnp.float32), axis=0)
    term = term[:share] + term[share:]
    swap = [(place, place ^ 1) for place in range(dom_size)]
    term = term + lax.ppermute(term, "dom", swap)

    back = spread(back_plan, tiles, grads.reshape(rep_size * wide, width), col_blocks, 2, True)
    mine, other = (half.reshape(dom_size // 2, rows, width) for half in back)
    other = lax.ppermute(other, "dom", swap)
    joined = pl.pallas_call(
        join_kernel,
        grid=(dom_size // 2,),
        out_shape=jax.ShapeDtypeStruct((dom_size // 2, wide, width), jnp.bfloat16),
        in_specs=[
            pl.BlockSpec((1, rows, width), lambda i: (i, 0, 0)),
            pl.BlockSpec((1, rows, width), lambda i: (i, 0, 0)),
            pl.BlockSpec((share, width), lambda i: (0, 0)),
        ],
        out_specs=pl.BlockSpec((1, wide, width), lambda i: (i, 0, 0)),
        compiler_params=params,
        name="join",
    )(mine, other, term)
    same_core = [list(range(core, dom_size, 2)) for core in range(2)]
    back_parts = lax.all_to_all(joined, "dom", 0, 0, axis_index_groups=same_core, tiled=True)
    grad_features, term_out = pl.pallas_call(
        last_kernel,
        out_shape=(
            jax.ShapeDtypeStruct((rows, width), jnp.bfloat16),
            jax.ShapeDtypeStruct((rep_size, share, width), jnp.float32),
        ),
        compiler_params=params,
        name="last",
    )(back_parts, weight)
    grad_weight = lax.all_to_all(term_out, "rep", 0, 0, tiled=True).reshape(width, width)
    return (output, grad_features, grad_weight)


def solution(mesh):
    placed = (
        P(("dom", "rep"), None),
        P(),
        P(("dom", "rep"), None),
        P("dom", "rep", None),
        P("dom", "rep", None),
        P("dom", "rep", None, None, None),
        P("dom", "rep"),
    )
    return jax.shard_map(
        body,
        mesh=mesh,
        in_specs=placed,
        out_specs=(P(("dom", "rep"), None), P(("dom", "rep"), None), P()),
        check_vma=False,
    )
```

```python
import functools

import jax
import jax.numpy as jnp
from jax import lax
from jax.experimental import pallas as pl
from jax.experimental.pallas import tpu as pltpu
from jax.sharding import PartitionSpec as P

BLOCK = 128
UNROLL = 16
SCOPE = 32 << 20


def pair_plan(key, place, pick, count, keys):
    slots = place.shape[0]
    slot = jnp.arange(slots, dtype=jnp.int32)
    live = slot < count
    key = jnp.where(live, key, keys)
    earlier = (key[:, None] == key[None, :]) & (slot[None, :] < slot[:, None])
    rank = jnp.sum(earlier, axis=1, dtype=jnp.int32)
    block = jnp.arange(keys, dtype=jnp.int32)
    per_block = jnp.sum(key[None, :] == block[:, None], axis=1, dtype=jnp.int32)
    pairs = (per_block + 1) // 2
    late = block >= keys // 2
    turns_first = (jnp.sum(jnp.where(late, 0, pairs)) + UNROLL - 1) // UNROLL
    turns_second = (jnp.sum(jnp.where(late, pairs, 0)) + UNROLL - 1) // UNROLL
    before = (block[None, :] < block[:, None]) & (late[None, :] == late[:, None])
    before = jnp.sum(jnp.where(before, pairs[None, :], 0), axis=1, dtype=jnp.int32)
    before += jnp.where(late, turns_first * UNROLL, 0)
    first = jnp.sum(jnp.where(key[:, None] == block[None, :], before[None, :], 0), axis=1, dtype=jnp.int32)
    position = jnp.where(live, 2 * first + rank, -1)
    half = jnp.arange(((slots + keys) // (2 * UNROLL) + 2) * UNROLL * 2, dtype=jnp.int32)
    hit = half[:, None] == position[None, :]
    tile = jnp.sum(jnp.where(hit, slot[None, :] - slots, 0), axis=1, dtype=jnp.int32) + slots
    picked = jnp.sum(jnp.where(hit, pick[None, :], 0), axis=1, dtype=jnp.int32)
    placed = jnp.sum(jnp.where(hit, place[None, :], 0), axis=1, dtype=jnp.int32)
    return jnp.stack([turns_first, turns_second]), tile, picked, placed


def spread_kernel(flipped, sources, turns_ref, tile_ref, pick_ref, place_ref, tiles_ref, *refs):
    source_refs, out_refs = refs[:sources], refs[sources:-3]
    total_ref, held_ref, sems = refs[-3:]
    slots = tiles_ref.shape[0]
    wide = 2 * UNROLL
    middle = turns_ref[0]
    stop = middle + turns_ref[1]

    @pl.loop(0, stop)
    def _(turn):
        for step in range(wide):
            slot = turn * wide + step
            tile = jnp.minimum(tile_ref[slot], slots - 1)
            pltpu.make_async_copy(tiles_ref.at[tile], held_ref.at[slot], sems.at[turn]).start()

    total_ref[...] = jnp.zeros_like(total_ref)

    def tile_of(slot):
        return held_ref[slot] * (tile_ref[slot] < slots).astype(jnp.bfloat16)

    def add_turns(start, end, source_ref):
        def rows_of(slot):
            return source_ref[pl.ds(pl.multiple_of(pick_ref[slot] * BLOCK, BLOCK), BLOCK), :]

        @pl.loop(start, end)
        def _(turn):
            window = pl.ds(turn * wide, wide)
            pltpu.make_async_copy(tiles_ref.at[pl.ds(0, wide)], held_ref.at[window], sems.at[turn]).wait()
            for step in range(UNROLL):
                first = turn * wide + 2 * step
                rows = jnp.concatenate([rows_of(first), rows_of(first + 1)], axis=0)
                tiles = [tile_of(first), tile_of(first + 1)]
                if flipped:
                    product = lax.dot_general(
                        jnp.concatenate(tiles, axis=0),
                        rows,
                        (((0,), (0,)), ((), ())),
                        preferred_element_type=jnp.float32,
                    )
                else:
                    product = jnp.dot(jnp.concatenate(tiles, axis=1), rows, preferred_element_type=jnp.float32)
                total_ref[place_ref[first]] += product

    if sources == 1:
        add_turns(0, stop, source_refs[0])
    else:
        add_turns(0, middle, source_refs[0])
        add_turns(middle, stop, source_refs[1])
    part = total_ref.shape[0] // len(out_refs)
    for i, out_ref in enumerate(out_refs):
        out_ref[...] = total_ref[i * part : (i + 1) * part].astype(out_ref.dtype)


def spread(plan, tiles, sources, places, out_types, flipped):
    width = sources[0].shape[1]
    halves = plan[1].shape[0]
    in_vmem = pl.BlockSpec(memory_space=pltpu.VMEM)
    part = places // len(out_types)
    return pl.pallas_call(
        functools.partial(spread_kernel, flipped, len(sources)),
        out_shape=[jax.ShapeDtypeStruct((part, BLOCK, width), out_type) for out_type in out_types],
        in_specs=[pl.BlockSpec(memory_space=pltpu.SMEM)] * 4
        + [pl.BlockSpec(memory_space=pltpu.HBM)]
        + [in_vmem] * len(sources),
        out_specs=[in_vmem] * len(out_types),
        scratch_shapes=[
            pltpu.VMEM((places, BLOCK, width), jnp.float32),
            pltpu.VMEM((halves, BLOCK, BLOCK), tiles.dtype),
            pltpu.SemaphoreType.DMA((halves // (2 * UNROLL),)),
        ],
        compiler_params=pltpu.CompilerParams(vmem_limit_bytes=SCOPE),
        cost_estimate=pl.CostEstimate(
            flops=2 * tiles.size * width, bytes_accessed=2 * (tiles.size + len(sources) * sources[0].size), transcendentals=0
        ),
        name="spread_back" if flipped else "spread_forward",
    )(*plan, tiles, *sources)


def split(value):
    high = value.astype(jnp.bfloat16)
    return high, (value - high.astype(jnp.float32)).astype(jnp.bfloat16)


def middle_kernel(parts_ref, weight_ref, cotangent_ref, out_ref, send_ref, term_ref):
    members = parts_ref.shape[0]
    mixed = parts_ref[0].astype(jnp.float32)
    for member in range(1, members):
        mixed += parts_ref[member].astype(jnp.float32)
    high, low = split(mixed)
    weight = weight_ref[...]
    summed = jnp.dot(high, weight, preferred_element_type=jnp.float32)
    summed += jnp.dot(low, weight, preferred_element_type=jnp.float32)
    sig = jax.nn.sigmoid(summed)
    out_ref[...] = (summed * sig).astype(out_ref.dtype)
    slope = sig * (1.0 + summed * (1.0 - sig))
    grad = (cotangent_ref[...].astype(jnp.float32) * slope).astype(jnp.bfloat16)
    across = (((0,), (0,)), ((), ()))
    term = lax.dot_general(high, grad, across, preferred_element_type=jnp.float32)
    term += lax.dot_general(low, grad, across, preferred_element_type=jnp.float32)
    term_ref[...] = term
    for member in range(members):
        send_ref[member] = grad


def join_kernel(own_ref, other_ref, term_ref, send_ref):
    rows = own_ref.shape[1]
    share = term_ref.shape[0]
    send_ref[0, :rows, :] = (own_ref[0] + other_ref[0].astype(jnp.float32)).astype(jnp.bfloat16)
    high, low = split(term_ref[...])
    send_ref[0, rows : rows + share, :] = high
    send_ref[0, rows + share :, :] = low


def last_kernel(parts_ref, weight_ref, out_ref, term_ref):
    members = parts_ref.shape[0]
    rows = out_ref.shape[0]
    share = term_ref.shape[0] // members
    total = parts_ref[0, :rows].astype(jnp.float32)
    for member in range(1, members):
        total += parts_ref[member, :rows].astype(jnp.float32)
    grad = total.astype(jnp.bfloat16)
    out_ref[...] = lax.dot_general(
        grad, weight_ref[...], (((1,), (1,)), ((), ())), preferred_element_type=jnp.float32
    ).astype(out_ref.dtype)
    for member in range(members):
        place = sum(((member >> bit) & 1) * (term_ref.shape[0] >> (bit + 1)) for bit in range(members.bit_length() - 1))
        high = parts_ref[member, rows : rows + share].astype(jnp.float32)
        term_ref[place : place + share, :] = high + parts_ref[member, rows + share :].astype(jnp.float32)


def exchange(value, axis, bit):
    size = lax.axis_size(axis)
    return lax.ppermute(value, axis, [(place, place ^ bit) for place in range(size)])


def halve(value, axis, bit):
    size = value.shape[0] // 2
    upper = (lax.axis_index(axis) & bit) != 0
    low, high = value[:size], value[size:]
    return jnp.where(upper, high, low) + exchange(jnp.where(upper, low, high), axis, bit)


def body(node_features, weight, cotangent, tile_row, tile_col, tile_values, tile_count):
    rows, width = node_features.shape
    dom_size = lax.axis_size("dom")
    rep_size = lax.axis_size("rep")
    slots = tile_row.shape[2]
    own = rows // BLOCK
    chips = dom_size // 2
    share = width // chips
    wide = rows + 2 * share
    params = pltpu.CompilerParams(vmem_limit_bytes=24 << 20)
    row_index = tile_row.reshape(slots)
    col_index = tile_col.reshape(slots)
    count = tile_count.reshape(())
    tiles = pltpu.with_memory_space_constraint(tile_values.reshape(slots, BLOCK, BLOCK), pltpu.HBM)
    parity = lax.axis_index("dom") % 2

    same_core = [list(range(core, dom_size, 2)) for core in range(2)]
    row_blocks = rep_size * own
    col_blocks = chips * own

    owner = col_index // own
    away = (owner + parity) % 2
    col_own = (owner // 2) * own + col_index % own
    forward_plan = pair_plan(
        away * row_blocks + row_index, row_index, col_own, count, 2 * row_blocks
    )
    col_place = away * col_blocks + col_own
    back_plan = pair_plan(col_place, col_place, row_index, count, 2 * col_blocks)

    copies = jnp.broadcast_to(node_features[None], (chips, rows, width))
    near = lax.all_to_all(copies, "dom", 0, 0, axis_index_groups=same_core, tiled=True)
    far = exchange(near, "dom", 1)
    near, far = near.reshape(chips * rows, width), far.reshape(chips * rows, width)
    (partial,) = spread(forward_plan, tiles, [near, far], row_blocks, [jnp.bfloat16], False)
    parts = lax.all_to_all(partial.reshape(rep_size, rows, width), "rep", 0, 0, tiled=True)
    output, grads, term = pl.pallas_call(
        middle_kernel,
        out_shape=(
            jax.ShapeDtypeStruct((rows, width), jnp.bfloat16),
            jax.ShapeDtypeStruct((rep_size, rows, width), jnp.bfloat16),
            jax.ShapeDtypeStruct((width, width), jnp.float32),
        ),
        compiler_params=params,
        name="middle",
    )(parts, weight, cotangent)
    grads = lax.all_to_all(grads, "rep", 0, 0, tiled=True).reshape(rep_size * rows, width)

    term = term + exchange(term, "dom", 1)
    bit = 2
    while bit < dom_size:
        term = halve(term, "dom", bit)
        bit *= 2
    bit = rep_size // 2
    term = term + exchange(term, "rep", bit)
    grads, term = lax.optimization_barrier((grads, term))

    bit //= 2
    term = term + exchange(term, "rep", bit)
    mine, other = spread(
        back_plan, tiles, [grads], 2 * col_blocks, [jnp.float32, jnp.bfloat16], True
    )
    mine, other = mine.reshape(chips, rows, width), other.reshape(chips, rows, width)
    other = exchange(other, "dom", 1)
    while bit > 1:
        bit //= 2
        term = term + exchange(term, "rep", bit)
    joined = pl.pallas_call(
        join_kernel,
        grid=(chips,),
        out_shape=jax.ShapeDtypeStruct((chips, wide, width), jnp.bfloat16),
        in_specs=[
            pl.BlockSpec((1, rows, width), lambda i: (i, 0, 0)),
            pl.BlockSpec((1, rows, width), lambda i: (i, 0, 0)),
            pl.BlockSpec((share, width), lambda i: (0, 0)),
        ],
        out_specs=pl.BlockSpec((1, wide, width), lambda i: (i, 0, 0)),
        compiler_params=params,
        name="join",
    )(mine, other, term)
    back_parts = lax.all_to_all(joined, "dom", 0, 0, axis_index_groups=same_core, tiled=True)
    grad_features, grad_weight = pl.pallas_call(
        last_kernel,
        out_shape=(
            jax.ShapeDtypeStruct((rows, width), jnp.bfloat16),
            jax.ShapeDtypeStruct((width, width), jnp.float32),
        ),
        compiler_params=params,
        name="last",
    )(back_parts, weight)
    return (output, grad_features, grad_weight)


def solution(mesh):
    placed = (
        P(("dom", "rep"), None),
        P(),
        P(("dom", "rep"), None),
        P("dom", "rep", None),
        P("dom", "rep", None),
        P("dom", "rep", None, None, None),
        P("dom", "rep"),
    )
    return jax.shard_map(
        body,
        mesh=mesh,
        in_specs=placed,
        out_specs=(P(("dom", "rep"), None), P(("dom", "rep"), None), P()),
        check_vma=False,
    )
```

```python
import functools

import jax
import jax.numpy as jnp
from jax import lax
from jax.experimental import pallas as pl
from jax.experimental.pallas import tpu as pltpu
from jax.sharding import PartitionSpec as P

BLOCK = 128
UNROLL = 16
SCOPE = 32 << 20


def pair_plan(key, place, pick, count, keys):
    slots = place.shape[0]
    slot = jnp.arange(slots, dtype=jnp.int32)
    live = slot < count
    key = jnp.where(live, key, keys)
    earlier = (key[:, None] == key[None, :]) & (slot[None, :] < slot[:, None])
    rank = jnp.sum(earlier, axis=1, dtype=jnp.int32)
    block = jnp.arange(keys, dtype=jnp.int32)
    per_block = jnp.sum(key[None, :] == block[:, None], axis=1, dtype=jnp.int32)
    pairs = (per_block + 1) // 2
    late = block >= keys // 2
    turns_first = (jnp.sum(jnp.where(late, 0, pairs)) + UNROLL - 1) // UNROLL
    turns_second = (jnp.sum(jnp.where(late, pairs, 0)) + UNROLL - 1) // UNROLL
    before = (block[None, :] < block[:, None]) & (late[None, :] == late[:, None])
    before = jnp.sum(jnp.where(before, pairs[None, :], 0), axis=1, dtype=jnp.int32)
    before += jnp.where(late, turns_first * UNROLL, 0)
    first = jnp.sum(jnp.where(key[:, None] == block[None, :], before[None, :], 0), axis=1, dtype=jnp.int32)
    position = jnp.where(live, 2 * first + rank, -1)
    half = jnp.arange(((slots + keys) // (2 * UNROLL) + 2) * UNROLL * 2, dtype=jnp.int32)
    hit = half[:, None] == position[None, :]
    tile = jnp.sum(jnp.where(hit, slot[None, :] - slots, 0), axis=1, dtype=jnp.int32) + slots
    picked = jnp.sum(jnp.where(hit, pick[None, :], 0), axis=1, dtype=jnp.int32)
    placed = jnp.sum(jnp.where(hit, place[None, :], 0), axis=1, dtype=jnp.int32)
    return jnp.stack([turns_first, turns_second]), tile, picked, placed


def spread_kernel(flipped, sources, turns_ref, tile_ref, pick_ref, place_ref, tiles_ref, *refs):
    source_refs, out_refs = refs[:sources], refs[sources:-3]
    total_ref, held_ref, sems = refs[-3:]
    slots = tiles_ref.shape[0]
    wide = 2 * UNROLL
    middle = turns_ref[0]
    stop = middle + turns_ref[1]

    @pl.loop(0, stop)
    def _(turn):
        for step in range(wide):
            slot = turn * wide + step
            tile = jnp.minimum(tile_ref[slot], slots - 1)
            pltpu.make_async_copy(tiles_ref.at[tile], held_ref.at[slot], sems.at[turn]).start()

    total_ref[...] = jnp.zeros_like(total_ref)

    def tile_of(slot):
        return held_ref[slot] * (tile_ref[slot] < slots).astype(jnp.bfloat16)

    def add_turns(start, end, source_ref):
        def rows_of(slot):
            return source_ref[pl.ds(pl.multiple_of(pick_ref[slot] * BLOCK, BLOCK), BLOCK), :]

        @pl.loop(start, end)
        def _(turn):
            window = pl.ds(turn * wide, wide)
            pltpu.make_async_copy(tiles_ref.at[pl.ds(0, wide)], held_ref.at[window], sems.at[turn]).wait()
            for step in range(UNROLL):
                first = turn * wide + 2 * step
                rows = jnp.concatenate([rows_of(first), rows_of(first + 1)], axis=0)
                tiles = [tile_of(first), tile_of(first + 1)]
                if flipped:
                    product = lax.dot_general(
                        jnp.concatenate(tiles, axis=0),
                        rows,
                        (((0,), (0,)), ((), ())),
                        preferred_element_type=jnp.float32,
                    )
                else:
                    product = jnp.dot(jnp.concatenate(tiles, axis=1), rows, preferred_element_type=jnp.float32)
                total_ref[place_ref[first]] += product

    if sources == 1:
        add_turns(0, stop, source_refs[0])
    else:
        add_turns(0, middle, source_refs[0])
        add_turns(middle, stop, source_refs[1])
    part = total_ref.shape[0] // len(out_refs)
    for i, out_ref in enumerate(out_refs):
        out_ref[...] = total_ref[i * part : (i + 1) * part].astype(out_ref.dtype)


def spread(plan, tiles, sources, places, out_types, flipped):
    width = sources[0].shape[1]
    halves = plan[1].shape[0]
    in_vmem = pl.BlockSpec(memory_space=pltpu.VMEM)
    part = places // len(out_types)
    return pl.pallas_call(
        functools.partial(spread_kernel, flipped, len(sources)),
        out_shape=[jax.ShapeDtypeStruct((part, BLOCK, width), out_type) for out_type in out_types],
        in_specs=[pl.BlockSpec(memory_space=pltpu.SMEM)] * 4
        + [pl.BlockSpec(memory_space=pltpu.HBM)]
        + [in_vmem] * len(sources),
        out_specs=[in_vmem] * len(out_types),
        scratch_shapes=[
            pltpu.VMEM((places, BLOCK, width), jnp.float32),
            pltpu.VMEM((halves, BLOCK, BLOCK), tiles.dtype),
            pltpu.SemaphoreType.DMA((halves // (2 * UNROLL),)),
        ],
        compiler_params=pltpu.CompilerParams(vmem_limit_bytes=SCOPE),
        cost_estimate=pl.CostEstimate(
            flops=2 * tiles.size * width, bytes_accessed=2 * (tiles.size + len(sources) * sources[0].size), transcendentals=0
        ),
        name="spread_back" if flipped else "spread_forward",
    )(*plan, tiles, *sources)


def split(value):
    high = value.astype(jnp.bfloat16)
    return high, (value - high.astype(jnp.float32)).astype(jnp.bfloat16)


def copies_kernel(value_ref, copies_ref, sems):
    copies = [pltpu.make_async_copy(value_ref, copies_ref.at[i], sems.at[i]) for i in range(copies_ref.shape[0])]
    for copy in copies:
        copy.start()
    for copy in copies:
        copy.wait()


def copies_of(value, members):
    return pl.pallas_call(
        copies_kernel,
        out_shape=pltpu.HBM((members, *value.shape), value.dtype),
        in_specs=[pl.BlockSpec(memory_space=pltpu.VMEM)],
        out_specs=pl.BlockSpec(memory_space=pltpu.HBM),
        scratch_shapes=[pltpu.SemaphoreType.DMA((members,))],
        name="copies",
    )(value)


def middle_kernel(parts_ref, weight_ref, cotangent_ref, out_ref, send_ref, term_ref, grad_ref, sems):
    members = parts_ref.shape[0]
    mixed = parts_ref[0].astype(jnp.float32)
    for member in range(1, members):
        mixed += parts_ref[member].astype(jnp.float32)
    high, low = split(mixed)
    weight = weight_ref[...]
    summed = jnp.dot(high, weight, preferred_element_type=jnp.float32)
    summed += jnp.dot(low, weight, preferred_element_type=jnp.float32)
    sig = jax.nn.sigmoid(summed)
    slope = sig * (1.0 + summed * (1.0 - sig))
    grad = (cotangent_ref[...].astype(jnp.float32) * slope).astype(jnp.bfloat16)
    grad_ref[...] = grad
    copies = [pltpu.make_async_copy(grad_ref, send_ref.at[i], sems.at[i]) for i in range(members)]
    for copy in copies:
        copy.start()
    out_ref[...] = (summed * sig).astype(out_ref.dtype)
    across = (((0,), (0,)), ((), ()))
    term = lax.dot_general(high, grad, across, preferred_element_type=jnp.float32)
    term += lax.dot_general(low, grad, across, preferred_element_type=jnp.float32)
    term_ref[...] = term
    for copy in copies:
        copy.wait()


def join_kernel(own_ref, other_ref, term_ref, send_ref):
    rows = own_ref.shape[1]
    send_ref[0, :rows, :] = (own_ref[0] + other_ref[0].astype(jnp.float32)).astype(jnp.bfloat16)
    send_ref[0, rows:, :] = term_ref[...].astype(jnp.bfloat16)


def last_kernel(parts_ref, weight_ref, out_ref, term_ref):
    members = parts_ref.shape[0]
    rows = out_ref.shape[0]
    share = parts_ref.shape[1] - rows
    pieces = term_ref.shape[0] // share
    grad = parts_ref[0, :rows].astype(jnp.float32)
    for member in range(1, members):
        grad += parts_ref[member, :rows].astype(jnp.float32)
    out_ref[...] = lax.dot_general(
        grad.astype(jnp.bfloat16), weight_ref[...], (((1,), (1,)), ((), ())), preferred_element_type=jnp.float32
    ).astype(out_ref.dtype)
    for piece in range(pieces):
        place = sum(((piece >> bit) & 1) * (term_ref.shape[0] >> (bit + 1)) for bit in range(pieces.bit_length() - 1))
        total = parts_ref[piece, rows:].astype(jnp.float32)
        for member in range(piece + pieces, members, pieces):
            total += parts_ref[member, rows:].astype(jnp.float32)
        term_ref[place : place + share, :] = total


def exchange(value, axis, bit):
    size = lax.axis_size(axis)
    return lax.ppermute(value, axis, [(place, place ^ bit) for place in range(size)])


def halve(value, axis, bit):
    size = value.shape[0] // 2
    upper = (lax.axis_index(axis) & bit) != 0
    low, high = value[:size], value[size:]
    return jnp.where(upper, high, low) + exchange(jnp.where(upper, low, high), axis, bit)


def body(node_features, weight, cotangent, tile_row, tile_col, tile_values, tile_count):
    rows, width = node_features.shape
    dom_size = lax.axis_size("dom")
    rep_size = lax.axis_size("rep")
    slots = tile_row.shape[2]
    own = rows // BLOCK
    chips = dom_size // 2
    pieces = chips // 2
    wide = rows + width // pieces
    params = pltpu.CompilerParams(vmem_limit_bytes=24 << 20)
    row_index = tile_row.reshape(slots)
    col_index = tile_col.reshape(slots)
    count = tile_count.reshape(())
    tiles = pltpu.with_memory_space_constraint(tile_values.reshape(slots, BLOCK, BLOCK), pltpu.HBM)
    parity = lax.axis_index("dom") % 2

    same_core = [list(range(core, dom_size, 2)) for core in range(2)]
    row_blocks = rep_size * own
    col_blocks = chips * own

    owner = col_index // own
    away = (owner + parity) % 2
    col_own = (owner // 2) * own + col_index % own
    forward_plan = pair_plan(
        away * row_blocks + row_index, row_index, col_own, count, 2 * row_blocks
    )
    col_place = away * col_blocks + col_own
    back_plan = pair_plan(col_place, col_place, row_index, count, 2 * col_blocks)

    near = lax.all_to_all(copies_of(node_features, chips), "dom", 0, 0, axis_index_groups=same_core, tiled=True)
    far = exchange(near, "dom", 1)
    near, far = near.reshape(chips * rows, width), far.reshape(chips * rows, width)
    (partial,) = spread(forward_plan, tiles, [near, far], row_blocks, [jnp.bfloat16], False)
    parts = lax.all_to_all(partial.reshape(rep_size, rows, width), "rep", 0, 0, tiled=True)
    in_vmem = pl.BlockSpec(memory_space=pltpu.VMEM)
    output, grads, term = pl.pallas_call(
        middle_kernel,
        out_shape=(
            jax.ShapeDtypeStruct((rows, width), jnp.bfloat16),
            pltpu.HBM((rep_size, rows, width), jnp.bfloat16),
            jax.ShapeDtypeStruct((width, width), jnp.float32),
        ),
        in_specs=[in_vmem] * 3,
        out_specs=(in_vmem, pl.BlockSpec(memory_space=pltpu.HBM), in_vmem),
        scratch_shapes=[pltpu.VMEM((rows, width), jnp.bfloat16), pltpu.SemaphoreType.DMA((rep_size,))],
        compiler_params=params,
        name="middle",
    )(parts, weight, cotangent)
    grads = lax.all_to_all(grads, "rep", 0, 0, tiled=True).reshape(rep_size * rows, width)

    bit = 2
    while bit <= pieces:
        term = halve(term, "dom", bit)
        bit *= 2
    term = term + exchange(term, "dom", 1)
    term = term + exchange(term, "rep", rep_size // 2)
    grads, term = lax.optimization_barrier((grads, term))

    mine, other = spread(
        back_plan, tiles, [grads], 2 * col_blocks, [jnp.float32, jnp.bfloat16], True
    )
    mine, other = mine.reshape(chips, rows, width), other.reshape(chips, rows, width)
    other = exchange(other, "dom", 1)
    term = (term + exchange(term, "rep", 2)) + (exchange(term, "rep", 1) + exchange(term, "rep", 3))
    joined = pl.pallas_call(
        join_kernel,
        grid=(chips,),
        out_shape=jax.ShapeDtypeStruct((chips, wide, width), jnp.bfloat16),
        in_specs=[
            pl.BlockSpec((1, rows, width), lambda i: (i, 0, 0)),
            pl.BlockSpec((1, rows, width), lambda i: (i, 0, 0)),
            pl.BlockSpec((width // pieces, width), lambda i: (0, 0)),
        ],
        out_specs=pl.BlockSpec((1, wide, width), lambda i: (i, 0, 0)),
        compiler_params=params,
        name="join",
    )(mine, other, term)
    back_parts = lax.all_to_all(joined, "dom", 0, 0, axis_index_groups=same_core, tiled=True)
    grad_features, grad_weight = pl.pallas_call(
        last_kernel,
        out_shape=(
            jax.ShapeDtypeStruct((rows, width), jnp.bfloat16),
            jax.ShapeDtypeStruct((width, width), jnp.float32),
        ),
        compiler_params=params,
        name="last",
    )(back_parts, weight)
    return (output, grad_features, grad_weight)


def solution(mesh):
    placed = (
        P(("dom", "rep"), None),
        P(),
        P(("dom", "rep"), None),
        P("dom", "rep", None),
        P("dom", "rep", None),
        P("dom", "rep", None, None, None),
        P("dom", "rep"),
    )
    return jax.shard_map(
        body,
        mesh=mesh,
        in_specs=placed,
        out_specs=(P(("dom", "rep"), None), P(("dom", "rep"), None), P()),
        check_vma=False,
    )
```

```python
import functools
import math

import jax
import jax.numpy as jnp
from jax import lax
from jax.experimental import pallas as pl
from jax.experimental.pallas import tpu as pltpu
from jax.sharding import PartitionSpec as P

BLOCK = 128
UNROLL = 16
SCOPE = 32 << 20


def pair_plan(key, place, pick, count, keys):
    slots = place.shape[0]
    slot = jnp.arange(slots, dtype=jnp.int32)
    live = slot < count
    key = jnp.where(live, key, keys)
    earlier = (key[:, None] == key[None, :]) & (slot[None, :] < slot[:, None])
    rank = jnp.sum(earlier, axis=1, dtype=jnp.int32)
    block = jnp.arange(keys, dtype=jnp.int32)
    per_block = jnp.sum(key[None, :] == block[:, None], axis=1, dtype=jnp.int32)
    pairs = (per_block + 1) // 2
    late = block >= keys // 2
    turns_first = (jnp.sum(jnp.where(late, 0, pairs)) + UNROLL - 1) // UNROLL
    turns_second = (jnp.sum(jnp.where(late, pairs, 0)) + UNROLL - 1) // UNROLL
    before = (block[None, :] < block[:, None]) & (late[None, :] == late[:, None])
    before = jnp.sum(jnp.where(before, pairs[None, :], 0), axis=1, dtype=jnp.int32)
    before += jnp.where(late, turns_first * UNROLL, 0)
    first = jnp.sum(jnp.where(key[:, None] == block[None, :], before[None, :], 0), axis=1, dtype=jnp.int32)
    position = jnp.where(live, 2 * first + rank, -1)
    half = jnp.arange(((slots + keys) // (2 * UNROLL) + 2) * UNROLL * 2, dtype=jnp.int32)
    hit = half[:, None] == position[None, :]
    tile = jnp.sum(jnp.where(hit, slot[None, :] - slots, 0), axis=1, dtype=jnp.int32) + slots
    picked = jnp.sum(jnp.where(hit, pick[None, :], 0), axis=1, dtype=jnp.int32)
    placed = jnp.sum(jnp.where(hit, place[None, :], 0), axis=1, dtype=jnp.int32)
    return jnp.stack([turns_first, turns_second]), tile, picked, placed


def spread_kernel(flipped, sources, turns_ref, tile_ref, pick_ref, place_ref, tiles_ref, *refs):
    source_refs, out_refs = refs[:sources], refs[sources:-3]
    total_ref, held_ref, sems = refs[-3:]
    slots = tiles_ref.shape[0]
    wide = 2 * UNROLL
    middle = turns_ref[0]
    stop = middle + turns_ref[1]

    @pl.loop(0, stop)
    def _(turn):
        for step in range(wide):
            slot = turn * wide + step
            tile = jnp.minimum(tile_ref[slot], slots - 1)
            pltpu.make_async_copy(tiles_ref.at[tile], held_ref.at[slot], sems.at[turn]).start()

    total_ref[...] = jnp.zeros_like(total_ref)

    def tile_of(slot):
        return held_ref[slot] * (tile_ref[slot] < slots).astype(jnp.bfloat16)

    def add_turns(start, end, source_ref):
        def rows_of(slot):
            return source_ref[pl.ds(pl.multiple_of(pick_ref[slot] * BLOCK, BLOCK), BLOCK), :]

        @pl.loop(start, end)
        def _(turn):
            window = pl.ds(turn * wide, wide)
            pltpu.make_async_copy(tiles_ref.at[pl.ds(0, wide)], held_ref.at[window], sems.at[turn]).wait()
            for step in range(UNROLL):
                first = turn * wide + 2 * step
                rows = jnp.concatenate([rows_of(first), rows_of(first + 1)], axis=0)
                tiles = [tile_of(first), tile_of(first + 1)]
                if flipped:
                    product = lax.dot_general(
                        jnp.concatenate(tiles, axis=0),
                        rows,
                        (((0,), (0,)), ((), ())),
                        preferred_element_type=jnp.float32,
                    )
                else:
                    product = jnp.dot(jnp.concatenate(tiles, axis=1), rows, preferred_element_type=jnp.float32)
                total_ref[place_ref[first]] += product

    if sources == 1:
        add_turns(0, stop, source_refs[0])
    else:
        add_turns(0, middle, source_refs[0])
        add_turns(middle, stop, source_refs[1])
    part = total_ref.shape[0] // len(out_refs)
    for i, out_ref in enumerate(out_refs):
        out_ref[...] = total_ref[i * part : (i + 1) * part].astype(out_ref.dtype)


def spread(plan, tiles, sources, places, out_types, flipped):
    width = sources[0].shape[1]
    halves = plan[1].shape[0]
    in_vmem = pl.BlockSpec(memory_space=pltpu.VMEM)
    part = places // len(out_types)
    return pl.pallas_call(
        functools.partial(spread_kernel, flipped, len(sources)),
        out_shape=[jax.ShapeDtypeStruct((part, BLOCK, width), out_type) for out_type in out_types],
        in_specs=[pl.BlockSpec(memory_space=pltpu.SMEM)] * 4
        + [pl.BlockSpec(memory_space=pltpu.HBM)]
        + [in_vmem] * len(sources),
        out_specs=[in_vmem] * len(out_types),
        scratch_shapes=[
            pltpu.VMEM((places, BLOCK, width), jnp.float32),
            pltpu.VMEM((halves, BLOCK, BLOCK), tiles.dtype),
            pltpu.SemaphoreType.DMA((halves // (2 * UNROLL),)),
        ],
        compiler_params=pltpu.CompilerParams(vmem_limit_bytes=SCOPE),
        cost_estimate=pl.CostEstimate(
            flops=2 * tiles.size * width, bytes_accessed=2 * (tiles.size + len(sources) * sources[0].size), transcendentals=0
        ),
        name="spread_back" if flipped else "spread_forward",
    )(*plan, tiles, *sources)


def split(value):
    high = value.astype(jnp.bfloat16)
    return high, (value - high.astype(jnp.float32)).astype(jnp.bfloat16)


def copies_kernel(value_ref, copies_ref, sems):
    copies = [pltpu.make_async_copy(value_ref, copies_ref.at[i], sems.at[i]) for i in range(copies_ref.shape[0])]
    for copy in copies:
        copy.start()
    for copy in copies:
        copy.wait()


def copies_of(value, members):
    return pl.pallas_call(
        copies_kernel,
        out_shape=pltpu.HBM((members, *value.shape), value.dtype),
        in_specs=[pl.BlockSpec(memory_space=pltpu.VMEM)],
        out_specs=pl.BlockSpec(memory_space=pltpu.HBM),
        scratch_shapes=[pltpu.SemaphoreType.DMA((members,))],
        name="copies",
    )(value)


def middle_kernel(parts_ref, weight_ref, cotangent_ref, out_ref, send_ref, term_ref, grad_ref, sems):
    members = parts_ref.shape[0]
    mixed = parts_ref[0].astype(jnp.float32)
    for member in range(1, members):
        mixed += parts_ref[member].astype(jnp.float32)
    high, low = split(mixed)
    weight = weight_ref[...]
    summed = jnp.dot(high, weight, preferred_element_type=jnp.float32)
    summed += jnp.dot(low, weight, preferred_element_type=jnp.float32)
    sig = jax.nn.sigmoid(summed)
    slope = sig * (1.0 + summed * (1.0 - sig))
    grad = (cotangent_ref[...].astype(jnp.float32) * slope).astype(jnp.bfloat16)
    grad_ref[...] = grad
    copies = [pltpu.make_async_copy(grad_ref, send_ref.at[i], sems.at[i]) for i in range(members)]
    for copy in copies:
        copy.start()
    out_ref[...] = (summed * sig).astype(out_ref.dtype)
    across = (((0,), (0,)), ((), ()))
    term = lax.dot_general(high, grad, across, preferred_element_type=jnp.float32)
    term += lax.dot_general(low, grad, across, preferred_element_type=jnp.float32)
    term_ref[...] = term
    for copy in copies:
        copy.wait()


def join_kernel(own_ref, other_ref, send_ref, sum_ref, sems):
    copies = [pltpu.make_async_copy(sum_ref.at[i], send_ref.at[i], sems.at[i]) for i in range(sum_ref.shape[0])]
    for i, copy in enumerate(copies):
        sum_ref[i] = (own_ref[i] + other_ref[i].astype(jnp.float32)).astype(jnp.bfloat16)
        copy.start()
    for copy in copies:
        copy.wait()


def last_kernel(parts_ref, weight_ref, out_ref):
    grad = parts_ref[0].astype(jnp.float32)
    for member in range(1, parts_ref.shape[0]):
        grad += parts_ref[member].astype(jnp.float32)
    out_ref[...] = lax.dot_general(
        grad.astype(jnp.bfloat16), weight_ref[...], (((1,), (1,)), ((), ())), preferred_element_type=jnp.float32
    ).astype(out_ref.dtype)


def ordered(value, other, axis, bit):
    upper = (lax.axis_index(axis) & bit) != 0
    return jnp.concatenate([jnp.where(upper, other, value), jnp.where(upper, value, other)], axis=0)


def exchange(value, axis, bit):
    size = math.prod(lax.axis_size(name) for name in ((axis,) if isinstance(axis, str) else axis))
    return lax.ppermute(value, axis, [(place, place ^ bit) for place in range(size)])


def halve(value, axis, bit):
    size = value.shape[0] // 2
    upper = (lax.axis_index(axis) & bit) != 0
    low, high = value[:size], value[size:]
    return jnp.where(upper, high, low) + exchange(jnp.where(upper, low, high), axis, bit)


def body(node_features, weight, cotangent, tile_row, tile_col, tile_values, tile_count):
    rows, width = node_features.shape
    dom_size = lax.axis_size("dom")
    rep_size = lax.axis_size("rep")
    slots = tile_row.shape[2]
    own = rows // BLOCK
    chips = dom_size // 2
    pieces = chips // 2
    params = pltpu.CompilerParams(vmem_limit_bytes=24 << 20)
    row_index = tile_row.reshape(slots)
    col_index = tile_col.reshape(slots)
    count = tile_count.reshape(())
    tiles = pltpu.with_memory_space_constraint(tile_values.reshape(slots, BLOCK, BLOCK), pltpu.HBM)
    parity = lax.axis_index("dom") % 2

    same_core = [list(range(core, dom_size, 2)) for core in range(2)]
    row_blocks = rep_size * own
    col_blocks = chips * own

    owner = col_index // own
    away = (owner + parity) % 2
    col_own = (owner // 2) * own + col_index % own
    forward_plan = pair_plan(
        away * row_blocks + row_index, row_index, col_own, count, 2 * row_blocks
    )
    col_place = away * col_blocks + col_own
    back_plan = pair_plan(col_place, col_place, row_index, count, 2 * col_blocks)

    near = lax.all_to_all(copies_of(node_features, chips), "dom", 0, 0, axis_index_groups=same_core, tiled=True)
    far = exchange(near, "dom", 1)
    near, far = near.reshape(chips * rows, width), far.reshape(chips * rows, width)
    (partial,) = spread(forward_plan, tiles, [near, far], row_blocks, [jnp.bfloat16], False)
    parts = lax.all_to_all(partial.reshape(rep_size, rows, width), "rep", 0, 0, tiled=True)
    in_vmem = pl.BlockSpec(memory_space=pltpu.VMEM)
    output, grads, term = pl.pallas_call(
        middle_kernel,
        out_shape=(
            jax.ShapeDtypeStruct((rows, width), jnp.bfloat16),
            pltpu.HBM((rep_size, rows, width), jnp.bfloat16),
            jax.ShapeDtypeStruct((width, width), jnp.float32),
        ),
        in_specs=[in_vmem] * 3,
        out_specs=(in_vmem, pl.BlockSpec(memory_space=pltpu.HBM), in_vmem),
        scratch_shapes=[pltpu.VMEM((rows, width), jnp.bfloat16), pltpu.SemaphoreType.DMA((rep_size,))],
        compiler_params=params,
        name="middle",
    )(parts, weight, cotangent)
    grads = lax.all_to_all(grads, "rep", 0, 0, tiled=True).reshape(rep_size * rows, width)

    bit = 2
    while bit <= pieces:
        term = halve(term, "dom", bit)
        bit *= 2
    term = term + exchange(term, "dom", 1)
    across = [("dom", "rep"), ("dom", dom_size // 2), ("rep", rep_size // 2)]
    both = exchange(term, across[0], (dom_size // 2) * rep_size + rep_size // 2)
    term = (term + exchange(term, *across[1])) + (exchange(term, *across[2]) + both)
    grads, term = lax.optimization_barrier((grads, term))

    mine, other = spread(
        back_plan, tiles, [grads], 2 * col_blocks, [jnp.float32, jnp.bfloat16], True
    )
    mine, other = mine.reshape(chips, rows, width), other.reshape(chips, rows, width)
    other = exchange(other, "dom", 1)
    joined = pl.pallas_call(
        join_kernel,
        out_shape=pltpu.HBM((chips, rows, width), jnp.bfloat16),
        in_specs=[in_vmem] * 2,
        out_specs=pl.BlockSpec(memory_space=pltpu.HBM),
        scratch_shapes=[pltpu.VMEM((chips, rows, width), jnp.bfloat16), pltpu.SemaphoreType.DMA((chips,))],
        compiler_params=params,
        name="join",
    )(mine, other)
    joined, term = lax.optimization_barrier((joined, term))
    back_parts = lax.all_to_all(joined, "dom", 0, 0, axis_index_groups=same_core, tiled=True)
    term = (term + exchange(term, "rep", 2)) + (exchange(term, "rep", 1) + exchange(term, "rep", 3))
    near_half = ordered(term, exchange(term, "dom", 4), "dom", 4)
    far_half = ordered(exchange(term, "dom", 2), exchange(term, "dom", 6), "dom", 4)
    grad_weight = ordered(near_half, far_half, "dom", 2)
    back_parts, grad_weight = lax.optimization_barrier((back_parts, grad_weight))
    grad_features = pl.pallas_call(
        last_kernel,
        out_shape=jax.ShapeDtypeStruct((rows, width), jnp.bfloat16),
        compiler_params=params,
        name="last",
    )(back_parts, weight)
    return (output, grad_features, grad_weight)


def solution(mesh):
    placed = (
        P(("dom", "rep"), None),
        P(),
        P(("dom", "rep"), None),
        P("dom", "rep", None),
        P("dom", "rep", None),
        P("dom", "rep", None, None, None),
        P("dom", "rep"),
    )
    return jax.shard_map(
        body,
        mesh=mesh,
        in_specs=placed,
        out_specs=(P(("dom", "rep"), None), P(("dom", "rep"), None), P()),
        check_vma=False,
    )
```

```python
import functools
import math

import jax
import jax.numpy as jnp
from jax import lax
from jax.experimental import pallas as pl
from jax.experimental.pallas import tpu as pltpu
from jax.sharding import PartitionSpec as P

BLOCK = 128
UNROLL = 16
SCOPE = 32 << 20


def pair_plan(key, place, pick, count, keys):
    slots = place.shape[0]
    slot = jnp.arange(slots, dtype=jnp.int32)
    live = slot < count
    key = jnp.where(live, key, keys)
    earlier = (key[:, None] == key[None, :]) & (slot[None, :] < slot[:, None])
    rank = jnp.sum(earlier, axis=1, dtype=jnp.int32)
    block = jnp.arange(keys, dtype=jnp.int32)
    per_block = jnp.sum(key[None, :] == block[:, None], axis=1, dtype=jnp.int32)
    pairs = (per_block + 1) // 2
    late = block >= keys // 2
    turns_first = (jnp.sum(jnp.where(late, 0, pairs)) + UNROLL - 1) // UNROLL
    turns_second = (jnp.sum(jnp.where(late, pairs, 0)) + UNROLL - 1) // UNROLL
    before = (block[None, :] < block[:, None]) & (late[None, :] == late[:, None])
    before = jnp.sum(jnp.where(before, pairs[None, :], 0), axis=1, dtype=jnp.int32)
    before += jnp.where(late, turns_first * UNROLL, 0)
    first = jnp.sum(jnp.where(key[:, None] == block[None, :], before[None, :], 0), axis=1, dtype=jnp.int32)
    position = jnp.where(live, 2 * first + rank, -1)
    half = jnp.arange(((slots + keys) // (2 * UNROLL) + 2) * UNROLL * 2, dtype=jnp.int32)
    hit = half[:, None] == position[None, :]
    tile = jnp.sum(jnp.where(hit, slot[None, :] - slots, 0), axis=1, dtype=jnp.int32) + slots
    picked = jnp.sum(jnp.where(hit, pick[None, :], 0), axis=1, dtype=jnp.int32)
    placed = jnp.sum(jnp.where(hit, place[None, :], 0), axis=1, dtype=jnp.int32)
    return jnp.stack([turns_first, turns_second]), tile, picked, placed


def spread_kernel(flipped, half, given, turns_ref, tile_ref, pick_ref, place_ref, tiles_ref, *refs):
    source_ref, out_ref = refs[0], refs[1 + given]
    total_ref, held_ref, sems = refs[-3:]
    slots = tiles_ref.shape[0]
    wide = 2 * UNROLL
    start = turns_ref[0] * half
    stop = start + turns_ref[half]

    @pl.loop(start, stop)
    def _(turn):
        for step in range(wide):
            slot = turn * wide + step
            tile = jnp.minimum(tile_ref[slot], slots - 1)
            pltpu.make_async_copy(tiles_ref.at[tile], held_ref.at[slot], sems.at[turn]).start()

    total_ref[...] = refs[1][...] if given else jnp.zeros_like(total_ref)

    def tile_of(slot):
        return held_ref[slot] * (tile_ref[slot] < slots).astype(jnp.bfloat16)

    def rows_of(slot):
        return source_ref[pl.ds(pl.multiple_of(pick_ref[slot] * BLOCK, BLOCK), BLOCK), :]

    @pl.loop(start, stop)
    def _(turn):
        window = pl.ds(turn * wide, wide)
        pltpu.make_async_copy(tiles_ref.at[pl.ds(0, wide)], held_ref.at[window], sems.at[turn]).wait()
        for step in range(UNROLL):
            first = turn * wide + 2 * step
            rows = jnp.concatenate([rows_of(first), rows_of(first + 1)], axis=0)
            tiles = [tile_of(first), tile_of(first + 1)]
            if flipped:
                product = lax.dot_general(
                    jnp.concatenate(tiles, axis=0), rows, (((0,), (0,)), ((), ())), preferred_element_type=jnp.float32
                )
            else:
                product = jnp.dot(jnp.concatenate(tiles, axis=1), rows, preferred_element_type=jnp.float32)
            total_ref[place_ref[first]] += product

    if total_ref is not out_ref:
        out_ref[...] = total_ref[...].astype(out_ref.dtype)


def spread(plan, half, tiles, source, places, given, out_type, flipped):
    width = source.shape[1]
    halves = plan[1].shape[0]
    in_vmem = pl.BlockSpec(memory_space=pltpu.VMEM)
    return pl.pallas_call(
        functools.partial(spread_kernel, flipped, half, len(given)),
        out_shape=jax.ShapeDtypeStruct((places, BLOCK, width), out_type),
        in_specs=[pl.BlockSpec(memory_space=pltpu.SMEM)] * 4
        + [pl.BlockSpec(memory_space=pltpu.HBM)]
        + [in_vmem] * (1 + len(given)),
        out_specs=in_vmem,
        scratch_shapes=[
            pltpu.VMEM((places, BLOCK, width), jnp.float32),
            pltpu.VMEM((halves, BLOCK, BLOCK), tiles.dtype),
            pltpu.SemaphoreType.DMA((halves // (2 * UNROLL),)),
        ],
        compiler_params=pltpu.CompilerParams(vmem_limit_bytes=SCOPE),
        cost_estimate=pl.CostEstimate(
            flops=tiles.size * width, bytes_accessed=tiles.size + 2 * source.size, transcendentals=0
        ),
        name=f"spread_{'back' if flipped else 'forward'}_{half}",
    )(*plan, tiles, source, *given)


def split(value):
    high = value.astype(jnp.bfloat16)
    return high, (value - high.astype(jnp.float32)).astype(jnp.bfloat16)


def copies_kernel(value_ref, copies_ref, sems):
    copies = [pltpu.make_async_copy(value_ref, copies_ref.at[i], sems.at[i]) for i in range(copies_ref.shape[0])]
    for copy in copies:
        copy.start()
    for copy in copies:
        copy.wait()


def copies_of(value, members):
    return pl.pallas_call(
        copies_kernel,
        out_shape=pltpu.HBM((members, *value.shape), value.dtype),
        in_specs=[pl.BlockSpec(memory_space=pltpu.VMEM)],
        out_specs=pl.BlockSpec(memory_space=pltpu.HBM),
        scratch_shapes=[pltpu.SemaphoreType.DMA((members,))],
        name="copies",
    )(value)


def middle_kernel(parts_ref, weight_ref, cotangent_ref, out_ref, send_ref, term_ref, grad_ref, sems):
    members = parts_ref.shape[0]
    mixed = parts_ref[0].astype(jnp.float32)
    for member in range(1, members):
        mixed += parts_ref[member].astype(jnp.float32)
    high, low = split(mixed)
    weight = weight_ref[...]
    summed = jnp.dot(high, weight, preferred_element_type=jnp.float32)
    summed += jnp.dot(low, weight, preferred_element_type=jnp.float32)
    sig = jax.nn.sigmoid(summed)
    slope = sig * (1.0 + summed * (1.0 - sig))
    grad = (cotangent_ref[...].astype(jnp.float32) * slope).astype(jnp.bfloat16)
    grad_ref[...] = grad
    copies = [pltpu.make_async_copy(grad_ref, send_ref.at[i], sems.at[i]) for i in range(members)]
    for copy in copies:
        copy.start()
    out_ref[...] = (summed * sig).astype(out_ref.dtype)
    across = (((0,), (0,)), ((), ()))
    term = lax.dot_general(high, grad, across, preferred_element_type=jnp.float32)
    term += lax.dot_general(low, grad, across, preferred_element_type=jnp.float32)
    term_ref[...] = term
    for copy in copies:
        copy.wait()


def join_kernel(own_ref, other_ref, send_ref, sum_ref, sems):
    copies = [pltpu.make_async_copy(sum_ref.at[i], send_ref.at[i], sems.at[i]) for i in range(sum_ref.shape[0])]
    for i, copy in enumerate(copies):
        sum_ref[i] = (own_ref[i] + other_ref[i].astype(jnp.float32)).astype(jnp.bfloat16)
        copy.start()
    for copy in copies:
        copy.wait()


def last_kernel(parts_ref, weight_ref, out_ref):
    grad = parts_ref[0].astype(jnp.float32)
    for member in range(1, parts_ref.shape[0]):
        grad += parts_ref[member].astype(jnp.float32)
    out_ref[...] = lax.dot_general(
        grad.astype(jnp.bfloat16), weight_ref[...], (((1,), (1,)), ((), ())), preferred_element_type=jnp.float32
    ).astype(out_ref.dtype)


def ordered(value, other, axis, bit):
    upper = (lax.axis_index(axis) & bit) != 0
    return jnp.concatenate([jnp.where(upper, other, value), jnp.where(upper, value, other)], axis=0)


def exchange(value, axis, bit):
    size = math.prod(lax.axis_size(name) for name in ((axis,) if isinstance(axis, str) else axis))
    return lax.ppermute(value, axis, [(place, place ^ bit) for place in range(size)])


def halve(value, axis, bit):
    size = value.shape[0] // 2
    upper = (lax.axis_index(axis) & bit) != 0
    low, high = value[:size], value[size:]
    return jnp.where(upper, high, low) + exchange(jnp.where(upper, low, high), axis, bit)


def body(node_features, weight, cotangent, tile_row, tile_col, tile_values, tile_count):
    rows, width = node_features.shape
    dom_size = lax.axis_size("dom")
    rep_size = lax.axis_size("rep")
    slots = tile_row.shape[2]
    own = rows // BLOCK
    chips = dom_size // 2
    pieces = chips // 2
    params = pltpu.CompilerParams(vmem_limit_bytes=24 << 20)
    row_index = tile_row.reshape(slots)
    col_index = tile_col.reshape(slots)
    count = tile_count.reshape(())
    tiles = pltpu.with_memory_space_constraint(tile_values.reshape(slots, BLOCK, BLOCK), pltpu.HBM)
    parity = lax.axis_index("dom") % 2

    same_core = [list(range(core, dom_size, 2)) for core in range(2)]
    row_blocks = rep_size * own
    col_blocks = chips * own

    owner = col_index // own
    away = (owner + parity) % 2
    col_own = (owner // 2) * own + col_index % own
    forward_plan = pair_plan(
        away * row_blocks + row_index, row_index, col_own, count, 2 * row_blocks
    )
    back_plan = pair_plan((1 - away) * col_blocks + col_own, col_own, row_index, count, 2 * col_blocks)

    near = lax.all_to_all(copies_of(node_features, chips), "dom", 0, 0, axis_index_groups=same_core, tiled=True)
    far = exchange(near, "dom", 1)
    near, far = near.reshape(chips * rows, width), far.reshape(chips * rows, width)
    partial = spread(forward_plan, 0, tiles, near, row_blocks, [], jnp.float32, False)
    partial = spread(forward_plan, 1, tiles, far, row_blocks, [partial], jnp.bfloat16, False)
    parts = lax.all_to_all(partial.reshape(rep_size, rows, width), "rep", 0, 0, tiled=True)
    in_vmem = pl.BlockSpec(memory_space=pltpu.VMEM)
    output, grads, term = pl.pallas_call(
        middle_kernel,
        out_shape=(
            jax.ShapeDtypeStruct((rows, width), jnp.bfloat16),
            pltpu.HBM((rep_size, rows, width), jnp.bfloat16),
            jax.ShapeDtypeStruct((width, width), jnp.float32),
        ),
        in_specs=[in_vmem] * 3,
        out_specs=(in_vmem, pl.BlockSpec(memory_space=pltpu.HBM), in_vmem),
        scratch_shapes=[pltpu.VMEM((rows, width), jnp.bfloat16), pltpu.SemaphoreType.DMA((rep_size,))],
        compiler_params=params,
        name="middle",
    )(parts, weight, cotangent)
    grads = lax.all_to_all(grads, "rep", 0, 0, tiled=True).reshape(rep_size * rows, width)

    bit = 2
    while bit <= pieces:
        term = halve(term, "dom", bit)
        bit *= 2
    term = term + exchange(term, "dom", 1)
    across = [("dom", "rep"), ("dom", dom_size // 2), ("rep", rep_size // 2)]
    both = exchange(term, across[0], (dom_size // 2) * rep_size + rep_size // 2)
    term = (term + exchange(term, *across[1])) + (exchange(term, *across[2]) + both)
    grads, term = lax.optimization_barrier((grads, term))

    other = spread(back_plan, 0, tiles, grads, col_blocks, [], jnp.bfloat16, True).reshape(chips, rows, width)
    other = exchange(other, "dom", 1)
    mine = spread(back_plan, 1, tiles, grads, col_blocks, [], jnp.float32, True).reshape(chips, rows, width)
    joined = pl.pallas_call(
        join_kernel,
        out_shape=pltpu.HBM((chips, rows, width), jnp.bfloat16),
        in_specs=[in_vmem] * 2,
        out_specs=pl.BlockSpec(memory_space=pltpu.HBM),
        scratch_shapes=[pltpu.VMEM((chips, rows, width), jnp.bfloat16), pltpu.SemaphoreType.DMA((chips,))],
        compiler_params=params,
        name="join",
    )(mine, other)
    joined, term = lax.optimization_barrier((joined, term))
    back_parts = lax.all_to_all(joined, "dom", 0, 0, axis_index_groups=same_core, tiled=True)
    term = (term + exchange(term, "rep", 2)) + (exchange(term, "rep", 1) + exchange(term, "rep", 3))
    near_half = ordered(term, exchange(term, "dom", 4), "dom", 4)
    far_half = ordered(exchange(term, "dom", 2), exchange(term, "dom", 6), "dom", 4)
    grad_weight = ordered(near_half, far_half, "dom", 2)
    back_parts, grad_weight = lax.optimization_barrier((back_parts, grad_weight))
    grad_features = pl.pallas_call(
        last_kernel,
        out_shape=jax.ShapeDtypeStruct((rows, width), jnp.bfloat16),
        compiler_params=params,
        name="last",
    )(back_parts, weight)
    return (output, grad_features, grad_weight)


def solution(mesh):
    placed = (
        P(("dom", "rep"), None),
        P(),
        P(("dom", "rep"), None),
        P("dom", "rep", None),
        P("dom", "rep", None),
        P("dom", "rep", None, None, None),
        P("dom", "rep"),
    )
    return jax.shard_map(
        body,
        mesh=mesh,
        in_specs=placed,
        out_specs=(P(("dom", "rep"), None), P(("dom", "rep"), None), P()),
        check_vma=False,
    )
```
